32 devices in a mesh: ep: 16 (over z, y, core), et: 2 (over x).
Axes of the slice: x: 2, y: 2, z: 4, core: 2. Of those that a mesh axis runs over, the one named last changes fastest.
Arguments:
- tokens: bfloat16 [64, 7168], P(('ep', 'et')), may hold values from -6 to 6
- expert_ids: int32 [64, 8], P('ep'), may hold values from 0 to 15, all different within a row; in each aligned block of 4 rows (0 to 3, 4 to 7, ...) at most 4 rows name the same one
- combine_numerators: int32 [64, 8], P('ep'), may hold values from 1 to 16
- expert_input: bfloat16 [16, 7168, 1024], P('ep', None, 'et'), may hold values from -0.0625 to 0.0625
- expert_output: bfloat16 [16, 1024, 7168], P('ep', 'et'), may hold values from -0.1875 to 0.1875
Outputs:
- combined: bfloat16 [64, 7168], P('ep', 'et')
The draws below stay inside these ranges and needn't reach their ends.
Inputs may be any that keep to these rules, and one draw needn't show every extreme that they name: `expert_ids`: each row names 8 different experts. Within each aligned block of 4 rows (the rows of one index of ep) no expert is named by more than 4 rows, and in every draw some block has an expert named by exactly 4 rows.
All inputs are finite; a program needn't handle non-finite values.
Results may differ from the reference program's by a relative error of at most 0.015.
Values may be sent and summed in bfloat16 or wider, within the bound.
A program may use at most 64 MiB of HBM per device.

```python
import math
import jax
import jax.numpy as jnp
import numpy as np
from jax import lax

D = 7168
FF = 1024
TOP = 8
GROUP = 4
TOKENS = 64
EXPERTS = 16
CAP = 4
N_EP = 16
N_ET = 2


def with_ends(array, stream_key, least, top_value):
    dims = array.shape
    spot = [jax.random.randint(jax.random.fold_in(stream_key, axis), (), 0, dims[axis]) for axis in range(len(dims))]
    array = array.at[tuple(spot)].set(least)
    longest = dims.index(max(dims))
    spot[longest] = (spot[longest] + 1) % dims[longest]
    return array.at[tuple(spot)].set(top_value)


def block_scale(stream_key, dims, cuts, least, largest):
    loudness, own = 1.0, jax.random.fold_in(stream_key, 6)
    for position, shards_of in cuts:
        steps = jnp.exp(jax.random.uniform(jax.random.fold_in(own, position), (shards_of,), jnp.float32, least / len(cuts), largest / len(cuts)))
        loudness = loudness * jnp.repeat(steps, dims[position] // shards_of).reshape([-1 if axis == position else 1 for axis in range(len(dims))])
    return loudness


def deal_out(key, own, number, rows, number_of, top, reach, skew):
    ranking = jax.random.permutation(key, number_of)
    packed, ordinary = portions_of(number_of, rows * top, reach, skew, True), portions_of(number_of, rows * top, reach, skew, False)
    places = jnp.arange(number_of)

    def named(sizes, turn):
        used = int((sizes > 0).sum())
        fixed = max(1, used // 4)
        moved = fixed + (places - fixed + turn * (used - fixed)) % max(1, number_of - fixed)
        return jnp.zeros((number_of,), jnp.int32).at[ranking[jnp.where(places < fixed, places, moved)]].set(jnp.asarray(sizes, jnp.int32))

    sizes = jnp.where(number % 4 == 0, named(packed, number // 4), named(ordinary, number - number // 4 - 1))
    mixed = jax.random.permutation(jax.random.fold_in(own, 3), number_of)
    source_of, taker = mixed[0:number_of // 2 * 2:2], mixed[1:number_of // 2 * 2:2]
    slack = jnp.minimum(sizes[source_of] - 1, reach - sizes[taker]) // 2
    slack = jnp.where((source_of == ranking[0]) | (taker == ranking[0]) | (sizes[taker] == 0), 0, jnp.maximum(slack, 0))
    moved = jax.random.randint(jax.random.fold_in(own, 4), (number_of // 2,), 0, 1 << 20) % (slack + 1)
    sizes = sizes.at[source_of].add(-moved).at[taker].add(moved)
    members = jnp.searchsorted(jnp.cumsum(sizes), jnp.arange(rows * top), side="right").astype(jnp.int32)
    grid = members.reshape(top, rows).T
    grid = grid[jax.random.permutation(jax.random.fold_in(own, 1), rows)]
    turn = jax.random.randint(jax.random.fold_in(own, 2), (rows, 1), 0, top)
    return jnp.take_along_axis(grid, (jnp.arange(top)[None, :] + turn) % top, axis=1)


def portions_of(number_of, total, limit, slope, full):
    loads = [(1 << 20) // math.isqrt(grade ** slope) + 1 for grade in range(1, number_of + 1)]
    largest = limit if full else min(limit, max(-(-total // number_of), total * loads[0] // sum(loads)))
    least = 1 if total - largest >= number_of - 1 else 0
    holding, rest = [largest] + [least] * (number_of - 1), total - largest - least * (number_of - 1)
    while rest > 0:
        free = [i for i in range(1, number_of) if holding[i] < largest] or [i for i in range(1, number_of) if holding[i] < limit]
        mass, budget = sum([loads[i] for i in free]), rest
        for i in free:
            more = min(limit - holding[i], max(1, budget * loads[i] // mass), rest)
            holding[i] = holding[i] + more
            rest = rest - more
    return np.array(holding)


def bell_draw(stream_key, shape, spread, limit, cuts=(), held_as=jnp.bfloat16):
    level = block_scale(stream_key, shape, cuts, -0.22, 0.18) if cuts else 1.0
    values = jax.random.normal(stream_key, shape, jnp.float32) * spread * level
    return jnp.minimum(jnp.maximum(values, -limit), limit).astype(held_as)


def setup_inputs(seed: int = 0) -> dict:
    key_of = jax.random.split(jax.random.key(seed), 6)
    tokens = bell_draw(key_of[0], (TOKENS, D), 1.0, 6.0, ((0, 32),))
    expert_ids_keys = jax.random.split(jax.random.fold_in(key_of[1], 1), TOKENS // GROUP)
    expert_ids_turns = jax.random.permutation(jax.random.fold_in(key_of[1], 3), TOKENS // GROUP)
    expert_ids = jax.vmap(lambda own, number: deal_out(jax.random.fold_in(key_of[1], 2), own, number, GROUP, EXPERTS, TOP, CAP, 2))(expert_ids_keys, expert_ids_turns).reshape((TOKENS, TOP))
    combine_numerators = with_ends(jax.random.randint(key_of[2], (TOKENS, TOP), 1, 17), jax.random.fold_in(key_of[2], 1), 1, 16).astype(jnp.int32)
    expert_input = bell_draw(key_of[3], (EXPERTS, D, FF), D ** -0.5, 0.0625, ((0, 16), (2, 2)))
    expert_output = bell_draw(key_of[4], (EXPERTS, FF, D), FF ** -0.5, 0.1875, ((0, 16), (1, 2)))
    return dict(tokens=tokens, expert_ids=expert_ids, combine_numerators=combine_numerators, expert_input=expert_input, expert_output=expert_output)


def reference(tokens, expert_ids, combine_numerators, expert_input, expert_output):
    numerators = combine_numerators.astype(jnp.float32)
    weights = 2.5 * numerators / jnp.sum(numerators, axis=1, keepdims=True)
    slot_count = N_EP * CAP
    hidden_width = FF // N_ET

    def expert_step(running, expert):
        matches = expert_ids == expert
        picked = jnp.any(matches, axis=1)
        expert_weight = jnp.sum(jnp.where(matches, weights, jnp.float32(0.0)), axis=1)
        indices = jnp.nonzero(picked, size=slot_count, fill_value=0)[0].astype(jnp.int32)
        usable = jnp.arange(slot_count, dtype=jnp.int32) < jnp.sum(picked.astype(jnp.int32))
        gathered = tokens[indices]
        input_proj = lax.dynamic_index_in_dim(expert_input, expert, 0, keepdims=False)
        output_proj = lax.dynamic_index_in_dim(expert_output, expert, 0, keepdims=False)
        projected = jnp.dot(gathered, input_proj, preferred_element_type=jnp.float32)
        hidden = jax.nn.silu(projected).astype(jnp.bfloat16)
        pieces = jnp.einsum("mbh,bhd->bmd",
                            hidden.reshape(slot_count, N_ET, hidden_width).astype(jnp.float32),
                            output_proj.reshape(N_ET, hidden_width, D).astype(jnp.float32),
                            precision=lax.Precision.HIGHEST)
        pieces = lax.optimization_barrier(pieces.astype(jnp.bfloat16)).astype(jnp.float32)
        expert_out = jnp.sum(pieces, axis=0)
        expert_out = lax.optimization_barrier(expert_out.astype(jnp.bfloat16)).astype(jnp.float32)
        scaled = expert_weight[indices][:, None] * expert_out
        addition = jnp.where(usable[:, None], scaled, jnp.float32(0.0))
        return running.at[indices].add(addition), None

    start = jnp.zeros((TOKENS, D), jnp.float32)
    total, _ = lax.scan(expert_step, start, jnp.arange(EXPERTS, dtype=jnp.int32))
    return total.astype(jnp.bfloat16)
```

```python
import functools

import jax
import jax.numpy as jnp
from jax import lax
from jax.experimental import pallas as pl
from jax.experimental.pallas import tpu as pltpu
from jax.sharding import PartitionSpec as P

MESH = pl.DeviceIdType.MESH
PAIR = 2
LANES = 128


def routed_layer(tokens, expert_ids, combine_numerators, expert_input, expert_output):
    ep_count = lax.axis_size("ep")
    group_rows = lax.all_gather(tokens, "et", axis=0, tiled=True)
    group_size = group_rows.shape[0]
    row_width = group_rows.shape[1]
    top_count = expert_ids.shape[1]
    capacity = 2 * max(1, group_size * top_count // ep_count)
    slot_total = ep_count * capacity
    numerators = combine_numerators.astype(jnp.float32)
    weights = 2.5 * numerators / jnp.sum(numerators, axis=1, keepdims=True)
    slot_expert = jnp.arange(ep_count, dtype=jnp.int32)
    matches = expert_ids[:, :, None] == slot_expert[None, None, :]
    picked = jnp.any(matches, axis=1).astype(jnp.int32)
    expert_weight = jnp.sum(jnp.where(matches, weights[:, :, None], jnp.float32(0.0)), axis=1)
    row = jnp.arange(group_size, dtype=jnp.int32)
    earlier = row[None, :] < row[:, None]
    slot_rank = jnp.sum(jnp.where(earlier[:, :, None], picked[None, :, :], 0), axis=1)
    placing = (slot_rank[:, :, None] == jnp.arange(capacity, dtype=jnp.int32)[None, None, :]) & (
        picked[:, :, None] > 0
    )
    placing = placing.reshape(group_size, slot_total)
    combiner = jnp.where(placing, jnp.repeat(expert_weight, capacity, axis=1), jnp.float32(0.0))
    outgoing = jnp.dot(
        placing.astype(jnp.bfloat16).T, group_rows, preferred_element_type=jnp.float32
    )
    outgoing = outgoing.astype(jnp.bfloat16).reshape(ep_count, capacity, row_width)
    incoming = lax.all_to_all(outgoing, "ep", split_axis=0, concat_axis=0, tiled=True)
    expert_rows = incoming.reshape(slot_total, row_width)
    input_proj = expert_input[0]
    output_proj = expert_output[0]
    projected = jnp.dot(expert_rows, input_proj, preferred_element_type=jnp.float32)
    hidden = jax.nn.silu(projected).astype(jnp.bfloat16)
    partial_out = jnp.dot(hidden, output_proj, preferred_element_type=jnp.float32)
    partial_out = partial_out.reshape(ep_count, capacity, output_proj.shape[1])
    expert_out = lax.psum_scatter(
        partial_out.astype(jnp.bfloat16), "et", scatter_dimension=2, tiled=True
    )
    share_width = expert_out.shape[2]
    returned = lax.all_to_all(expert_out, "ep", split_axis=0, concat_axis=0, tiled=True)
    returned = returned.reshape(slot_total, share_width).astype(jnp.float32)
    combined = jnp.dot(
        combiner, returned, precision=lax.Precision.HIGHEST, preferred_element_type=jnp.float32
    )
    return combined.astype(jnp.bfloat16)


def fused_kernel(
    line,
    ids_hbm,
    numerators_hbm,
    tokens_hbm,
    input_hbm,
    output_hbm,
    out_ref,
    ids_ref,
    numerators_ref,
    rows,
    input_proj,
    output_proj,
    part,
    core_in,
    core_sum,
    first_a,
    first_b,
    second_a,
    second_b,
    last_a,
    last_b,
    line_out,
    line_in,
    weight_sem,
    own_sem,
    gather_send,
    gather_recv,
    reduce_send,
    reduce_recv,
    line_send,
    line_recv,
):
    ep, x = lax.axis_index("ep"), lax.axis_index("et")
    c, y, z = ep % PAIR, (ep // PAIR) % PAIR, ep // (PAIR * PAIR)
    group, top = ids_ref.shape
    share, width = tokens_hbm.shape
    half = width // 2
    quarter = half // 2
    depth = input_hbm.shape[2]
    experts = line * PAIR * PAIR

    def at(c=c, y=y, z=z, x=x):
        return {"ep": (z * PAIR + y) * PAIR + c, "et": x}

    to_core, to_y, to_x = at(c=1 - c), at(y=1 - y), at(x=1 - x)
    z_ahead = [lax.rem(z + step, line) for step in range(line)]
    z_behind = [lax.rem(z + line - step, line) for step in range(line)]

    barrier = pltpu.get_barrier_semaphore()
    partners = [to_core, to_y, to_x] + [at(z=z_ahead[step]) for step in range(1, line)]
    for partner in partners:
        pl.semaphore_signal(barrier, inc=1, device_id=partner, device_id_type=MESH)

    small = [
        pltpu.make_async_copy(ids_hbm, ids_ref, own_sem.at[2]),
        pltpu.make_async_copy(numerators_hbm, numerators_ref, own_sem.at[3]),
    ]
    for load in small:
        load.start()
    loads = [
        pltpu.make_async_copy(
            tokens_hbm.at[:, pl.ds(h * half, half)],
            rows.at[c, y, z, x, h, :, pl.ds(0, half)],
            own_sem.at[h],
        )
        for h in range(2)
    ]
    for load in loads:
        load.start()
    input_load = pltpu.make_async_copy(input_hbm.at[0], input_proj, weight_sem.at[0])
    input_load.start(priority=1)
    chunk_loads = []
    for hx in range(2):
        for p in range(2):
            load = pltpu.make_async_copy(
                output_hbm.at[0, :, pl.ds((2 * hx + p) * quarter, quarter)],
                output_proj.at[hx, p],
                weight_sem.at[1 + 2 * hx + p],
            )
            load.start(priority=1)
            chunk_loads.append(load)

    for load in small:
        load.wait()
    ids = ids_ref[...]
    numerators = numerators_ref[...]
    lane = lax.broadcasted_iota(jnp.int32, (group, LANES), 1)
    table = jnp.zeros((group, LANES), jnp.int32)
    for k in range(top):
        table = table + jnp.where(ids[:, k : k + 1] == lane, numerators[:, k : k + 1], 0)
    table = table.astype(jnp.float32)
    mine = table[:share]
    for step in range(1, group // share):
        mine = jnp.where(x == step, table[step * share : (step + 1) * share], mine)
    mine = mine.astype(jnp.bfloat16)
    for h in range(2):
        rows[c, y, z, x, h, :, half:] = mine

    for load in loads:
        load.wait()
    pl.semaphore_wait(barrier, len(partners))

    pending = []

    def send(src, dst, send_sem, recv_sem, partner):
        copy = pltpu.make_async_remote_copy(
            src_ref=src,
            dst_ref=dst,
            send_sem=send_sem,
            recv_sem=recv_sem,
            device_id=partner,
            device_id_type=MESH,
        )
        copy.start()
        pending.append(copy)

    def share_rows(slot, kind, step, partner):
        send(slot, slot, gather_send.at[kind, step], gather_recv.at[kind, step], partner)

    def arrived(slot, kind, step):
        pltpu.make_async_remote_copy(
            src_ref=slot,
            dst_ref=slot,
            send_sem=gather_send.at[kind, step],
            recv_sem=gather_recv.at[kind, step],
            device_id=to_core,
            device_id_type=MESH,
        ).wait_recv()

    own = rows.at[c, y, z, x]
    for step in range(1, line):
        share_rows(own, 0, step, at(z=z_ahead[step]))
    order = [0] + sorted(range(1, line), key=lambda step: min(step, line - step))
    for step in order:
        block = rows.at[c, y, z_behind[step], x]
        if step:
            arrived(block, 0, step)
        share_rows(block, 1, step, to_x)
        share_rows(block, 2, step, to_y)
        share_rows(block, 5, step, to_core)
    for step in order:
        zz = z_behind[step]
        block = rows.at[c, y, zz, 1 - x]
        arrived(block, 1, step)
        share_rows(block.at[0], 3, step, to_y)
        share_rows(block, 6, step, to_core)
        block = rows.at[c, 1 - y, zz, x]
        arrived(block, 2, step)
        share_rows(block.at[1], 4, step, to_x)
        share_rows(block, 7, step, to_core)
    for step in order:
        zz = z_behind[step]
        block = rows.at[c, 1 - y, zz, 1 - x]
        arrived(block.at[0], 3, step)
        share_rows(block.at[0], 8, step, to_core)
        arrived(block.at[1], 4, step)
        share_rows(block.at[1], 9, step, to_core)
    for step in order:
        zz = z_behind[step]
        arrived(rows.at[1 - c, y, zz, x], 5, step)
        arrived(rows.at[1 - c, y, zz, 1 - x], 6, step)
        arrived(rows.at[1 - c, 1 - y, zz, x], 7, step)
        arrived(rows.at[1 - c, 1 - y, zz, 1 - x, 0], 8, step)
        arrived(rows.at[1 - c, 1 - y, zz, 1 - x, 1], 9, step)

    token_count = experts * group
    table = rows[:, :, :, :, 0, :, half:].reshape(token_count, LANES).astype(jnp.float32)
    lane = lax.broadcasted_iota(jnp.int32, (token_count, LANES), 1)
    picked = jnp.sum(jnp.where(lane == ep, table, 0.0), axis=1, keepdims=True)
    weight = 2.5 * picked / jnp.sum(table, axis=1, keepdims=True)

    input_load.wait()
    projected = jnp.zeros((token_count, depth), jnp.float32)
    for h in range(2):
        taken = rows[:, :, :, :, h, :, :half].reshape(token_count, half)
        projected = projected + jnp.dot(
            taken, input_proj[h * half : (h + 1) * half, :], preferred_element_type=jnp.float32
        )
    hidden = jax.nn.silu(projected).astype(jnp.bfloat16)
    for load in chunk_loads:
        load.wait()

    line_rows = line * group
    f32 = jnp.float32

    def compute_chunk(hx, p):
        value = jnp.dot(hidden, output_proj[hx, p], preferred_element_type=jnp.float32)
        value = (value * weight).astype(jnp.bfloat16)
        for cc in range(PAIR):
            for yy in range(PAIR):
                start = (cc * PAIR + yy) * line_rows
                part[cc, yy, hx, p] = value[start : start + line_rows]

    def reduce_pair(index):
        return dict(send_sem=reduce_send.at[index], recv_sem=reduce_recv.at[index])

    def landed(slot, index):
        pltpu.make_async_remote_copy(
            src_ref=slot,
            dst_ref=slot,
            device_id=to_core,
            device_id_type=MESH,
            **reduce_pair(index),
        ).wait_recv()

    def send_chunk(index, hx, p):
        send(part.at[1 - c, :, hx, p], core_in.at[:, hx, p], partner=to_core, **reduce_pair(index))

    def add_chunk(index, hx, p):
        landed(core_in.at[:, hx, p], index)
        core_sum[:, hx, p] = (
            part[c, :, hx, p].astype(f32) + core_in[:, hx, p].astype(f32)
        ).astype(jnp.bfloat16)

    chunks = [(1 - x, 0), (x, 1), (1 - x, 1), (x, 0)]
    for index, (hx, p) in enumerate(chunks):
        compute_chunk(hx, p)
        send_chunk(index, hx, p)
    add_chunk(0, *chunks[0])
    send(core_sum.at[:, 1 - x, 0], first_a, partner=to_x, **reduce_pair(4))
    add_chunk(1, *chunks[1])
    add_chunk(2, *chunks[2])
    send(core_sum.at[1 - y, :, 1], first_b, partner=to_y, **reduce_pair(5))
    add_chunk(3, *chunks[3])

    landed(first_a, 4)
    second_a[...] = (core_sum[:, x, 0].astype(f32) + first_a[...].astype(f32)).astype(jnp.bfloat16)
    send(second_a.at[1 - y], last_a, partner=to_y, **reduce_pair(6))
    landed(first_b, 5)
    second_b[...] = (core_sum[y, :, 1].astype(f32) + first_b[...].astype(f32)).astype(jnp.bfloat16)
    send(second_b.at[1 - x], last_b, partner=to_x, **reduce_pair(7))

    def finish(p, value):
        for zz in range(line):
            line_out[zz, p] = value[zz * group : (zz + 1) * group].astype(jnp.bfloat16)
        for step in range(1, line):
            zz = z_ahead[step]
            send(
                line_out.at[zz, p],
                line_in.at[step, p],
                line_send.at[p, step],
                line_recv.at[p, step],
                at(z=zz),
            )

    landed(last_a, 6)
    finish(0, second_a[y].astype(f32) + last_a[...].astype(f32))
    landed(last_b, 7)
    finish(1, second_b[x].astype(f32) + last_b[...].astype(f32))
    for p in range(2):
        total = line_out[z, p].astype(f32)
        for step in range(1, line):
            slot = line_in.at[step, p]
            pltpu.make_async_remote_copy(
                src_ref=slot,
                dst_ref=slot,
                send_sem=line_send.at[p, step],
                recv_sem=line_recv.at[p, step],
                device_id=to_core,
                device_id_type=MESH,
            ).wait_recv()
            total = total + line_in[step, p].astype(f32)
        out_ref[:, p * quarter : (p + 1) * quarter] = total.astype(jnp.bfloat16)
    for copy in pending:
        copy.wait_send()


def fused_layer(tokens, expert_ids, combine_numerators, expert_input, expert_output):
    line = lax.axis_size("ep") // (PAIR * PAIR)
    share, width = tokens.shape
    group = expert_ids.shape[0]
    half, quarter = width // 2, width // 4
    depth = expert_input.shape[2]
    line_rows = line * group
    bf16 = jnp.bfloat16
    dma = pltpu.SemaphoreType.DMA
    vmem = pl.BlockSpec(memory_space=pltpu.VMEM)
    stay = pl.BlockSpec(memory_space=pl.ANY)
    return pl.pallas_call(
        functools.partial(fused_kernel, line),
        out_shape=pltpu.VMEM((group, half), bf16),
        in_specs=[stay] * 5,
        out_specs=vmem,
        scratch_shapes=[
            pltpu.VMEM(expert_ids.shape, expert_ids.dtype),
            pltpu.VMEM(combine_numerators.shape, combine_numerators.dtype),
            pltpu.VMEM((PAIR, PAIR, line, 2, 2, share, half + LANES), bf16),
            pltpu.VMEM((width, depth), bf16),
            pltpu.VMEM((2, 2, depth, quarter), bf16),
            pltpu.VMEM((PAIR, PAIR, 2, 2, line_rows, quarter), bf16),
            pltpu.VMEM((PAIR, 2, 2, line_rows, quarter), bf16),
            pltpu.VMEM((PAIR, 2, 2, line_rows, quarter), bf16),
            pltpu.VMEM((PAIR, line_rows, quarter), bf16),
            pltpu.VMEM((2, line_rows, quarter), bf16),
            pltpu.VMEM((PAIR, line_rows, quarter), bf16),
            pltpu.VMEM((2, line_rows, quarter), bf16),
            pltpu.VMEM((line_rows, quarter), bf16),
            pltpu.VMEM((line_rows, quarter), bf16),
            pltpu.VMEM((line, 2, group, quarter), bf16),
            pltpu.VMEM((line, 2, group, quarter), bf16),
            dma((5,)),
            dma((4,)),
            dma((10, line)),
            dma((10, line)),
            dma((8,)),
            dma((8,)),
            dma((2, line)),
            dma((2, line)),
        ],
        compiler_params=pltpu.CompilerParams(
            collective_id=0, has_side_effects=True, vmem_limit_bytes=60 * 1024 * 1024
        ),
    )(expert_ids, combine_numerators, tokens, expert_input, expert_output)


def per_device(tokens, expert_ids, combine_numerators, expert_input, expert_output):
    ep_count, et_count = lax.axis_size("ep"), lax.axis_size("et")
    group, top = expert_ids.shape
    capacity = 2 * max(1, group * top // ep_count)
    dense = group <= capacity and et_count == 2 and ep_count % (PAIR * PAIR) == 0
    run = fused_layer if dense and ep_count <= LANES else routed_layer
    return run(tokens, expert_ids, combine_numerators, expert_input, expert_output)


def solution(mesh):
    in_specs = (
        P(("ep", "et"), None),
        P("ep", None),
        P("ep", None),
        P("ep", None, "et"),
        P("ep", "et", None),
    )
    out_specs = P("ep", "et")
    return jax.shard_map(
        per_device, mesh=mesh, in_specs=in_specs, out_specs=out_specs, check_vma=False
    )
```

```python
import functools

import jax
import jax.numpy as jnp
from jax import lax
from jax.experimental import pallas as pl
from jax.experimental.pallas import tpu as pltpu
from jax.sharding import PartitionSpec as P

MESH = pl.DeviceIdType.MESH
PAIR = 2
LANES = 128


def routed_layer(tokens, expert_ids, combine_numerators, expert_input, expert_output):
    ep_count = lax.axis_size("ep")
    group_rows = lax.all_gather(tokens, "et", axis=0, tiled=True)
    group_size = group_rows.shape[0]
    row_width = group_rows.shape[1]
    top_count = expert_ids.shape[1]
    capacity = 2 * max(1, group_size * top_count // ep_count)
    slot_total = ep_count * capacity
    numerators = combine_numerators.astype(jnp.float32)
    weights = 2.5 * numerators / jnp.sum(numerators, axis=1, keepdims=True)
    slot_expert = jnp.arange(ep_count, dtype=jnp.int32)
    matches = expert_ids[:, :, None] == slot_expert[None, None, :]
    picked = jnp.any(matches, axis=1).astype(jnp.int32)
    expert_weight = jnp.sum(jnp.where(matches, weights[:, :, None], jnp.float32(0.0)), axis=1)
    row = jnp.arange(group_size, dtype=jnp.int32)
    earlier = row[None, :] < row[:, None]
    slot_rank = jnp.sum(jnp.where(earlier[:, :, None], picked[None, :, :], 0), axis=1)
    placing = (slot_rank[:, :, None] == jnp.arange(capacity, dtype=jnp.int32)[None, None, :]) & (
        picked[:, :, None] > 0
    )
    placing = placing.reshape(group_size, slot_total)
    combiner = jnp.where(placing, jnp.repeat(expert_weight, capacity, axis=1), jnp.float32(0.0))
    outgoing = jnp.dot(
        placing.astype(jnp.bfloat16).T, group_rows, preferred_element_type=jnp.float32
    )
    outgoing = outgoing.astype(jnp.bfloat16).reshape(ep_count, capacity, row_width)
    incoming = lax.all_to_all(outgoing, "ep", split_axis=0, concat_axis=0, tiled=True)
    expert_rows = incoming.reshape(slot_total, row_width)
    input_proj = expert_input[0]
    output_proj = expert_output[0]
    projected = jnp.dot(expert_rows, input_proj, preferred_element_type=jnp.float32)
    hidden = jax.nn.silu(projected).astype(jnp.bfloat16)
    partial_out = jnp.dot(hidden, output_proj, preferred_element_type=jnp.float32)
    partial_out = partial_out.reshape(ep_count, capacity, output_proj.shape[1])
    expert_out = lax.psum_scatter(
        partial_out.astype(jnp.bfloat16), "et", scatter_dimension=2, tiled=True
    )
    share_width = expert_out.shape[2]
    returned = lax.all_to_all(expert_out, "ep", split_axis=0, concat_axis=0, tiled=True)
    returned = returned.reshape(slot_total, share_width).astype(jnp.float32)
    combined = jnp.dot(
        combiner, returned, precision=lax.Precision.HIGHEST, preferred_element_type=jnp.float32
    )
    return combined.astype(jnp.bfloat16)


def fused_kernel(
    line,
    size,
    ids_hbm,
    numerators_hbm,
    tokens_hbm,
    input_hbm,
    output_hbm,
    out_ref,
    ids_ref,
    numerators_ref,
    rows,
    input_proj,
    output_proj,
    part,
    core_in,
    core_sum,
    plane_in,
    line_out,
    line_in,
    weight_sem,
    own_sem,
    gather_send,
    gather_recv,
    core_send,
    core_recv,
    plane_send,
    plane_recv,
    line_send,
    line_recv,
):
    ep, x = lax.axis_index("ep"), lax.axis_index("et")
    c, y, z = ep % PAIR, (ep // PAIR) % PAIR, ep // (PAIR * PAIR)
    group, top = ids_ref.shape
    share, width = tokens_hbm.shape
    quarter = width // 4
    depth = input_hbm.shape[2]
    f32, bf16 = jnp.float32, jnp.bfloat16

    def at(c=c, y=y, z=z, x=x):
        return {"ep": (z * PAIR + y) * PAIR + c, "et": x}

    def across(step):
        place, bit = z, 1
        while bit <= step:
            if step & bit:
                place = place + bit - 2 * bit * ((z // bit) % 2)
            bit *= 2
        return place

    to_core, to_y, to_x, to_diagonal = at(c=1 - c), at(y=1 - y), at(x=1 - x), at(y=1 - y, x=1 - x)
    steps = range(1, line)
    z_of = {step: across(step) for step in steps}
    to_line = {step: at(z=z_of[step]) for step in steps}

    barrier = pltpu.get_barrier_semaphore()
    partners = [to_core, to_y, to_x, to_diagonal] + list(to_line.values())
    for partner in partners:
        pl.semaphore_signal(barrier, inc=1, device_id=partner, device_id_type=MESH)

    def slot(plane, c=c, y=y, x=x):
        return rows.at[plane // size, c, y, plane % size, x]

    own = slot(z)
    small = [
        pltpu.make_async_copy(ids_hbm, ids_ref, own_sem.at[0]),
        pltpu.make_async_copy(numerators_hbm, numerators_ref, own_sem.at[1]),
    ]
    load_own = pltpu.make_async_copy(tokens_hbm, own.at[:, pl.ds(LANES, width)], own_sem.at[2])
    for load in small + [load_own]:
        load.start()
    input_load = pltpu.make_async_copy(input_hbm.at[0], input_proj, weight_sem.at[0])
    input_load.start(priority=1)
    chunk_loads = []
    for hx in range(2):
        for p in range(2):
            load = pltpu.make_async_copy(
                output_hbm.at[0, :, pl.ds((2 * hx + p) * quarter, quarter)],
                output_proj.at[hx, p],
                weight_sem.at[1 + 2 * hx + p],
            )
            load.start(priority=1)
            chunk_loads.append(load)

    for load in small:
        load.wait()
    ids = ids_ref[...]
    numerators = numerators_ref[...]
    lane = lax.broadcasted_iota(jnp.int32, (group, LANES), 1)
    table = jnp.zeros((group, LANES), jnp.int32)
    for k in range(top):
        table = table + jnp.where(ids[:, k : k + 1] == lane, numerators[:, k : k + 1], 0)
    table = table.astype(f32)
    mine = table[:share]
    for step in range(1, group // share):
        mine = jnp.where(x == step, table[step * share : (step + 1) * share], mine)
    rows[z // size, c, y, z % size, x, :, :LANES] = mine.astype(bf16)

    load_own.wait()
    pl.semaphore_wait(barrier, len(partners))

    pending = []

    def send(src, dst, send_sem, recv_sem, partner):
        copy = pltpu.make_async_remote_copy(
            src_ref=src,
            dst_ref=dst,
            send_sem=send_sem,
            recv_sem=recv_sem,
            device_id=partner,
            device_id_type=MESH,
        )
        copy.start()
        return copy

    def sent(*copy):
        pending.append(send(*copy))

    def landed(block, send_sem, recv_sem):
        pltpu.make_async_remote_copy(
            src_ref=block,
            dst_ref=block,
            send_sem=send_sem,
            recv_sem=recv_sem,
            device_id=to_core,
            device_id_type=MESH,
        ).wait_recv()

    def gather_pair(kind, step):
        return gather_send.at[kind, step], gather_recv.at[kind, step]

    def spread(step):
        block = slot(step)
        for kind, partner in ((1, to_x), (2, to_y), (3, to_diagonal), (4, to_core)):
            sent(block, block, *gather_pair(kind, step), partner)

    def from_line(step):
        landed(slot(z_of[step]), *gather_pair(0, z_of[step]))
        spread(z_of[step])

    def to_other_core(step):
        for kind, block in (
            (1, slot(step, x=1 - x)),
            (2, slot(step, y=1 - y)),
            (3, slot(step, y=1 - y, x=1 - x)),
        ):
            landed(block, *gather_pair(kind, step))
            sent(block, block, *gather_pair(kind + 4, step), to_core)

    def gathered(step):
        for kind, block in (
            (4, slot(step, c=1 - c)),
            (5, slot(step, c=1 - c, x=1 - x)),
            (6, slot(step, c=1 - c, y=1 - y)),
            (7, slot(step, c=1 - c, y=1 - y, x=1 - x)),
        ):
            landed(block, *gather_pair(kind, step))

    count = line // size
    block_rows = size * group
    token_count = count * PAIR * PAIR * block_rows
    chunks = [(1 - x, 0), (x, 0), (1 - x, 1), (x, 1)]

    def compute():
        table = rows[..., :LANES].reshape(token_count, LANES).astype(f32)
        lane = lax.broadcasted_iota(jnp.int32, (token_count, LANES), 1)
        picked = jnp.sum(jnp.where(lane == ep, table, 0.0), axis=1, keepdims=True)
        weight = 2.5 * picked / jnp.sum(table, axis=1, keepdims=True)
        input_load.wait()
        taken = rows[..., LANES:].reshape(token_count, width)
        projected = jnp.dot(taken, input_proj[...], preferred_element_type=f32)
        hidden = jax.nn.silu(projected).astype(bf16)
        for load in chunk_loads:
            load.wait()
        for index, (hx, p) in enumerate(chunks):
            value = jnp.dot(hidden, output_proj[hx, p], preferred_element_type=f32)
            value = (value * weight).astype(bf16)
            for b in range(count):
                for cc in range(PAIR):
                    for yy in range(PAIR):
                        start = ((b * PAIR + cc) * PAIR + yy) * block_rows
                        part[b, cc, hx, p, yy] = value[start : start + block_rows]
            for b in range(count):
                sent(
                    part.at[b, 1 - c, hx, p],
                    core_in.at[b, hx, p],
                    core_send.at[b, hx, p],
                    core_recv.at[b, hx, p],
                    to_core,
                )

    def add_cores(b):
        for index, (hx, p) in enumerate(chunks):
            landed(core_in.at[b, hx, p], core_send.at[b, hx, p], core_recv.at[b, hx, p])
            core_sum[b, hx, p] = (
                part[b, c, hx, p].astype(f32) + core_in[b, hx, p].astype(f32)
            ).astype(bf16)
            wants = ((0, y, to_x), (1, 1 - y, to_diagonal)) if index % 2 == 0 else ((2, 1 - y, to_y),)
            for kind, yy, partner in wants:
                sent(
                    core_sum.at[b, hx, p, yy],
                    plane_in.at[b, kind, p],
                    plane_send.at[b, kind, p],
                    plane_recv.at[b, kind, p],
                    partner,
                )

    def add_plane(b, p):
        total = core_sum[b, x, p, y].astype(f32)
        for kind in range(3):
            landed(plane_in.at[b, kind, p], plane_send.at[b, kind, p], plane_recv.at[b, kind, p])
            total = total + plane_in[b, kind, p].astype(f32)
        for i in range(size):
            plane = b * size + i
            line_out[plane, p] = total[i * group : (i + 1) * group].astype(bf16)

            @pl.when(plane != z)
            def _():
                home(plane, p).start()

    def home(plane, p):
        return pltpu.make_async_remote_copy(
            src_ref=line_out.at[plane, p],
            dst_ref=line_in.at[z, p],
            send_sem=line_send.at[plane, p],
            recv_sem=line_recv.at[z, p],
            device_id=at(z=plane),
            device_id_type=MESH,
        )

    for step in (2, 3, 1):
        sent(own, own, gather_send.at[0, step], gather_recv.at[0, z], to_line[step])
    spread(z)
    for step in (1, 2, 3):
        from_line(step)
    for step in (0, 1, 2, 3):
        to_other_core(z_of.get(step, z))
    for step in (0, 1, 2, 3):
        gathered(z_of.get(step, z))
    compute()

    add_cores(0)
    add_cores(1)
    for b in range(2):
        for p in range(2):
            add_plane(b, p)
    for p in range(2):
        total = line_out[z, p].astype(f32)
        for step in (1, 2, 3):
            other = z_of[step]
            landed(line_in.at[other, p], line_send.at[other, p], line_recv.at[other, p])
            total = total + line_in[other, p].astype(f32)
        out_ref[:, p * quarter : (p + 1) * quarter] = total.astype(bf16)
    for copy in pending:
        copy.wait_send()
    for step in steps:
        for p in range(2):
            home(z_of[step], p).wait_send()


def fused_layer(tokens, expert_ids, combine_numerators, expert_input, expert_output):
    line = lax.axis_size("ep") // (PAIR * PAIR)
    share, width = tokens.shape
    group = expert_ids.shape[0]
    half, quarter = width // 2, width // 4
    depth = expert_input.shape[2]
    count = 2
    size = line // count
    block_rows = size * group
    bf16 = jnp.bfloat16
    dma = pltpu.SemaphoreType.DMA
    stay = pl.BlockSpec(memory_space=pl.ANY)
    return pl.pallas_call(
        functools.partial(fused_kernel, line, size),
        out_shape=pltpu.VMEM((group, half), bf16),
        in_specs=[stay] * 5,
        out_specs=pl.BlockSpec(memory_space=pltpu.VMEM),
        scratch_shapes=[
            pltpu.VMEM(expert_ids.shape, expert_ids.dtype),
            pltpu.VMEM(combine_numerators.shape, combine_numerators.dtype),
            pltpu.VMEM((count, PAIR, PAIR, size, 2, share, LANES + width), bf16),
            pltpu.VMEM((width, depth), bf16),
            pltpu.VMEM((2, 2, depth, quarter), bf16),
            pltpu.VMEM((count, PAIR, 2, 2, PAIR, block_rows, quarter), bf16),
            pltpu.VMEM((count, 2, 2, PAIR, block_rows, quarter), bf16),
            pltpu.VMEM((count, 2, 2, PAIR, block_rows, quarter), bf16),
            pltpu.VMEM((count, 3, 2, block_rows, quarter), bf16),
            pltpu.VMEM((line, 2, group, quarter), bf16),
            pltpu.VMEM((line, 2, group, quarter), bf16),
            dma((5,)),
            dma((3,)),
            dma((8, line)),
            dma((8, line)),
            dma((count, 2, 2)),
            dma((count, 2, 2)),
            dma((count, 3, 2)),
            dma((count, 3, 2)),
            dma((line, 2)),
            dma((line, 2)),
        ],
        compiler_params=pltpu.CompilerParams(
            collective_id=0, has_side_effects=True, vmem_limit_bytes=60 * 1024 * 1024
        ),
    )(expert_ids, combine_numerators, tokens, expert_input, expert_output)


def per_device(tokens, expert_ids, combine_numerators, expert_input, expert_output):
    ep_count, et_count = lax.axis_size("ep"), lax.axis_size("et")
    group, top = expert_ids.shape
    capacity = 2 * max(1, group * top // ep_count)
    dense = group <= capacity and et_count == 2 and ep_count % (PAIR * PAIR) == 0
    run = fused_layer if dense and ep_count <= LANES else routed_layer
    return run(tokens, expert_ids, combine_numerators, expert_input, expert_output)


def solution(mesh):
    in_specs = (
        P(("ep", "et"), None),
        P("ep", None),
        P("ep", None),
        P("ep", None, "et"),
        P("ep", "et", None),
    )
    out_specs = P("ep", "et")
    return jax.shard_map(
        per_device, mesh=mesh, in_specs=in_specs, out_specs=out_specs, check_vma=False
    )
```

```python
import functools

import jax
import jax.numpy as jnp
from jax import lax
from jax.experimental import pallas as pl
from jax.experimental.pallas import tpu as pltpu
from jax.sharding import PartitionSpec as P

MESH = pl.DeviceIdType.MESH
PAIR = 2
LANES = 128


def routed_layer(tokens, expert_ids, combine_numerators, expert_input, expert_output):
    ep_count = lax.axis_size("ep")
    group_rows = lax.all_gather(tokens, "et", axis=0, tiled=True)
    group_size = group_rows.shape[0]
    row_width = group_rows.shape[1]
    top_count = expert_ids.shape[1]
    capacity = 2 * max(1, group_size * top_count // ep_count)
    slot_total = ep_count * capacity
    numerators = combine_numerators.astype(jnp.float32)
    weights = 2.5 * numerators / jnp.sum(numerators, axis=1, keepdims=True)
    slot_expert = jnp.arange(ep_count, dtype=jnp.int32)
    matches = expert_ids[:, :, None] == slot_expert[None, None, :]
    picked = jnp.any(matches, axis=1).astype(jnp.int32)
    expert_weight = jnp.sum(jnp.where(matches, weights[:, :, None], jnp.float32(0.0)), axis=1)
    row = jnp.arange(group_size, dtype=jnp.int32)
    earlier = row[None, :] < row[:, None]
    slot_rank = jnp.sum(jnp.where(earlier[:, :, None], picked[None, :, :], 0), axis=1)
    placing = (slot_rank[:, :, None] == jnp.arange(capacity, dtype=jnp.int32)[None, None, :]) & (
        picked[:, :, None] > 0
    )
    placing = placing.reshape(group_size, slot_total)
    combiner = jnp.where(placing, jnp.repeat(expert_weight, capacity, axis=1), jnp.float32(0.0))
    outgoing = jnp.dot(
        placing.astype(jnp.bfloat16).T, group_rows, preferred_element_type=jnp.float32
    )
    outgoing = outgoing.astype(jnp.bfloat16).reshape(ep_count, capacity, row_width)
    incoming = lax.all_to_all(outgoing, "ep", split_axis=0, concat_axis=0, tiled=True)
    expert_rows = incoming.reshape(slot_total, row_width)
    input_proj = expert_input[0]
    output_proj = expert_output[0]
    projected = jnp.dot(expert_rows, input_proj, preferred_element_type=jnp.float32)
    hidden = jax.nn.silu(projected).astype(jnp.bfloat16)
    partial_out = jnp.dot(hidden, output_proj, preferred_element_type=jnp.float32)
    partial_out = partial_out.reshape(ep_count, capacity, output_proj.shape[1])
    expert_out = lax.psum_scatter(
        partial_out.astype(jnp.bfloat16), "et", scatter_dimension=2, tiled=True
    )
    share_width = expert_out.shape[2]
    returned = lax.all_to_all(expert_out, "ep", split_axis=0, concat_axis=0, tiled=True)
    returned = returned.reshape(slot_total, share_width).astype(jnp.float32)
    combined = jnp.dot(
        combiner, returned, precision=lax.Precision.HIGHEST, preferred_element_type=jnp.float32
    )
    return combined.astype(jnp.bfloat16)


def fused_kernel(
    line,
    size,
    ids_hbm,
    numerators_hbm,
    tokens_hbm,
    input_hbm,
    output_hbm,
    out_ref,
    ids_ref,
    numerators_ref,
    rows,
    input_proj,
    output_proj,
    part,
    core_in,
    core_sum,
    plane_in,
    line_out,
    line_in,
    weight_sem,
    own_sem,
    gather_send,
    gather_recv,
    core_send,
    core_recv,
    plane_send,
    plane_recv,
    line_send,
    line_recv,
):
    ep, x = lax.axis_index("ep"), lax.axis_index("et")
    c, y, z = ep % PAIR, (ep // PAIR) % PAIR, ep // (PAIR * PAIR)
    group, top = ids_ref.shape
    share, width = tokens_hbm.shape
    quarter = width // 4
    depth = input_hbm.shape[2]
    f32, bf16 = jnp.float32, jnp.bfloat16

    def at(c=c, y=y, z=z, x=x):
        return {"ep": (z * PAIR + y) * PAIR + c, "et": x}

    def across(step):
        place, bit = z, 1
        while bit <= step:
            if step & bit:
                place = place + bit - 2 * bit * ((z // bit) % 2)
            bit *= 2
        return place

    to_core, to_y, to_x, to_diagonal = at(c=1 - c), at(y=1 - y), at(x=1 - x), at(y=1 - y, x=1 - x)
    steps = range(1, line)
    z_of = {step: across(step) for step in steps}
    to_line = {step: at(z=z_of[step]) for step in steps}

    barrier = pltpu.get_barrier_semaphore()
    partners = [to_core, to_y, to_x, to_diagonal] + list(to_line.values())
    for partner in partners:
        pl.semaphore_signal(barrier, inc=1, device_id=partner, device_id_type=MESH)

    def slot(plane, c=c, y=y, x=x):
        return rows.at[plane // size, c, y, plane % size, x]

    own = slot(z)
    small = [
        pltpu.make_async_copy(ids_hbm, ids_ref, own_sem.at[0]),
        pltpu.make_async_copy(numerators_hbm, numerators_ref, own_sem.at[1]),
    ]
    load_own = pltpu.make_async_copy(tokens_hbm, own.at[:, pl.ds(LANES, width)], own_sem.at[2])
    for load in small + [load_own]:
        load.start()
    input_load = pltpu.make_async_copy(input_hbm.at[0], input_proj, weight_sem.at[0])
    input_load.start(priority=1)
    chunk_loads = []
    for hx in range(2):
        for p in range(2):
            load = pltpu.make_async_copy(
                output_hbm.at[0, :, pl.ds((2 * hx + p) * quarter, quarter)],
                output_proj.at[hx, p],
                weight_sem.at[1 + 2 * hx + p],
            )
            load.start(priority=1)
            chunk_loads.append(load)

    for load in small:
        load.wait()
    ids = ids_ref[...]
    numerators = numerators_ref[...]
    lane = lax.broadcasted_iota(jnp.int32, (group, LANES), 1)
    table = jnp.zeros((group, LANES), jnp.int32)
    for k in range(top):
        table = table + jnp.where(ids[:, k : k + 1] == lane, numerators[:, k : k + 1], 0)
    table = table.astype(f32)
    mine = table[:share]
    for step in range(1, group // share):
        mine = jnp.where(x == step, table[step * share : (step + 1) * share], mine)
    rows[z // size, c, y, z % size, x, :, :LANES] = mine.astype(bf16)

    load_own.wait()
    pl.semaphore_wait(barrier, len(partners))

    pending = []

    def send(src, dst, send_sem, recv_sem, partner):
        copy = pltpu.make_async_remote_copy(
            src_ref=src,
            dst_ref=dst,
            send_sem=send_sem,
            recv_sem=recv_sem,
            device_id=partner,
            device_id_type=MESH,
        )
        copy.start()
        return copy

    def sent(*copy):
        pending.append(send(*copy))

    def landed(block, send_sem, recv_sem):
        pltpu.make_async_remote_copy(
            src_ref=block,
            dst_ref=block,
            send_sem=send_sem,
            recv_sem=recv_sem,
            device_id=to_core,
            device_id_type=MESH,
        ).wait_recv()

    def gather_pair(kind, step):
        return gather_send.at[kind, step], gather_recv.at[kind, step]

    def spread(step):
        block = slot(step)
        for kind, partner in ((3, to_diagonal), (1, to_x), (2, to_y), (4, to_core)):
            sent(block, block, *gather_pair(kind, step), partner)

    def from_line(step):
        landed(slot(z_of[step]), *gather_pair(0, z_of[step]))
        spread(z_of[step])

    def to_other_core(step):
        for kind, block in (
            (1, slot(step, x=1 - x)),
            (2, slot(step, y=1 - y)),
            (3, slot(step, y=1 - y, x=1 - x)),
        ):
            landed(block, *gather_pair(kind, step))
            sent(block, block, *gather_pair(kind + 4, step), to_core)

    def gathered(step):
        for kind, block in (
            (4, slot(step, c=1 - c)),
            (5, slot(step, c=1 - c, x=1 - x)),
            (6, slot(step, c=1 - c, y=1 - y)),
            (7, slot(step, c=1 - c, y=1 - y, x=1 - x)),
        ):
            landed(block, *gather_pair(kind, step))

    count = line // size
    block_rows = size * group
    token_count = count * PAIR * PAIR * block_rows
    chunks = [(1 - x, 0), (x, 0), (1 - x, 1), (x, 1)]

    def compute():
        table = rows[..., :LANES].reshape(token_count, LANES).astype(f32)
        lane = lax.broadcasted_iota(jnp.int32, (token_count, LANES), 1)
        picked = jnp.sum(jnp.where(lane == ep, table, 0.0), axis=1, keepdims=True)
        weight = 2.5 * picked / jnp.sum(table, axis=1, keepdims=True)
        input_load.wait()
        taken = rows[..., LANES:].reshape(token_count, width)
        projected = jnp.dot(taken, input_proj[...], preferred_element_type=f32)
        hidden = jax.nn.silu(projected).astype(bf16)
        for load in chunk_loads:
            load.wait()
        for index, (hx, p) in enumerate(chunks):
            value = jnp.dot(hidden, output_proj[hx, p], preferred_element_type=f32)
            value = (value * weight).astype(bf16)
            for b in range(count):
                for cc in range(PAIR):
                    for yy in range(PAIR):
                        start = ((b * PAIR + cc) * PAIR + yy) * block_rows
                        part[b, cc, hx, p, yy] = value[start : start + block_rows]
            sent(
                part.at[:, 1 - c, hx, p],
                core_in.at[:, hx, p],
                core_send.at[0, hx, p],
                core_recv.at[0, hx, p],
                to_core,
            )

    def add_cores(b):
        for index, (hx, p) in enumerate(chunks):
            if b == 0:
                landed(core_in.at[:, hx, p], core_send.at[0, hx, p], core_recv.at[0, hx, p])
            core_sum[b, hx, p] = (
                part[b, c, hx, p].astype(f32) + core_in[b, hx, p].astype(f32)
            ).astype(bf16)
            wants = ((1, 1 - y, to_diagonal), (0, y, to_x)) if index % 2 == 0 else ((2, 1 - y, to_y),)
            for kind, yy, partner in wants:
                sent(
                    core_sum.at[b, hx, p, yy],
                    plane_in.at[b, kind, p],
                    plane_send.at[b, kind, p],
                    plane_recv.at[b, kind, p],
                    partner,
                )

    def add_plane(b, p):
        total = core_sum[b, x, p, y].astype(f32)
        for kind in range(3):
            landed(plane_in.at[b, kind, p], plane_send.at[b, kind, p], plane_recv.at[b, kind, p])
            total = total + plane_in[b, kind, p].astype(f32)
        for i in range(size):
            plane = b * size + i
            line_out[plane, p] = total[i * group : (i + 1) * group].astype(bf16)

            @pl.when(plane != z)
            def _():
                home(plane, p).start()

    def home(plane, p):
        return pltpu.make_async_remote_copy(
            src_ref=line_out.at[plane, p],
            dst_ref=line_in.at[z, p],
            send_sem=line_send.at[plane, p],
            recv_sem=line_recv.at[z, p],
            device_id=at(z=plane),
            device_id_type=MESH,
        )

    low = (2 * z < line).astype(jnp.int32)
    for k in range(line - 1):
        value = line - 1 - k
        down, up = value - (value <= z).astype(jnp.int32), k + (k >= z).astype(jnp.int32)
        far = low * down + (1 - low) * up
        sent(own, own, gather_send.at[0, k], gather_recv.at[0, z], at(z=far))
    spread(z)
    near = [z] + [z_of[step] for step in steps]
    for step in steps:
        from_line(step)
    for plane in near:
        to_other_core(plane)
    for plane in near:
        gathered(plane)
    compute()
    for b in range(count):
        add_cores(b)
    for b in range(count):
        for p in range(2):
            add_plane(b, p)
    for p in range(2):
        total = line_out[z, p].astype(f32)
        for step in steps:
            other = z_of[step]
            landed(line_in.at[other, p], line_send.at[other, p], line_recv.at[other, p])
            total = total + line_in[other, p].astype(f32)
        out_ref[:, p * quarter : (p + 1) * quarter] = total.astype(bf16)
    for copy in pending:
        copy.wait_send()
    for step in steps:
        for p in range(2):
            home(z_of[step], p).wait_send()


def fused_layer(tokens, expert_ids, combine_numerators, expert_input, expert_output):
    line = lax.axis_size("ep") // (PAIR * PAIR)
    share, width = tokens.shape
    group = expert_ids.shape[0]
    half, quarter = width // 2, width // 4
    depth = expert_input.shape[2]
    count, size = line, 1
    block_rows = size * group
    bf16 = jnp.bfloat16
    dma = pltpu.SemaphoreType.DMA
    stay = pl.BlockSpec(memory_space=pl.ANY)
    return pl.pallas_call(
        functools.partial(fused_kernel, line, size),
        out_shape=pltpu.VMEM((group, half), bf16),
        in_specs=[stay] * 5,
        out_specs=pl.BlockSpec(memory_space=pltpu.VMEM),
        scratch_shapes=[
            pltpu.VMEM(expert_ids.shape, expert_ids.dtype),
            pltpu.VMEM(combine_numerators.shape, combine_numerators.dtype),
            pltpu.VMEM((count, PAIR, PAIR, size, 2, share, LANES + width), bf16),
            pltpu.VMEM((width, depth), bf16),
            pltpu.VMEM((2, 2, depth, quarter), bf16),
            pltpu.VMEM((count, PAIR, 2, 2, PAIR, block_rows, quarter), bf16),
            pltpu.VMEM((count, 2, 2, PAIR, block_rows, quarter), bf16),
            pltpu.VMEM((count, 2, 2, PAIR, block_rows, quarter), bf16),
            pltpu.VMEM((count, 3, 2, block_rows, quarter), bf16),
            pltpu.VMEM((line, 2, group, quarter), bf16),
            pltpu.VMEM((line, 2, group, quarter), bf16),
            dma((5,)),
            dma((3,)),
            dma((8, line)),
            dma((8, line)),
            dma((count, 2, 2)),
            dma((count, 2, 2)),
            dma((count, 3, 2)),
            dma((count, 3, 2)),
            dma((line, 2)),
            dma((line, 2)),
        ],
        compiler_params=pltpu.CompilerParams(
            collective_id=0, has_side_effects=True, vmem_limit_bytes=60 * 1024 * 1024
        ),
    )(expert_ids, combine_numerators, tokens, expert_input, expert_output)


def per_device(tokens, expert_ids, combine_numerators, expert_input, expert_output):
    ep_count, et_count = lax.axis_size("ep"), lax.axis_size("et")
    group, top = expert_ids.shape
    capacity = 2 * max(1, group * top // ep_count)
    line = ep_count // (PAIR * PAIR)
    dense = group <= capacity and et_count == 2 and ep_count == PAIR * PAIR * line
    dense = dense and line > 1 and line & (line - 1) == 0
    run = fused_layer if dense and ep_count <= LANES else routed_layer
    return run(tokens, expert_ids, combine_numerators, expert_input, expert_output)


def solution(mesh):
    in_specs = (
        P(("ep", "et"), None),
        P("ep", None),
        P("ep", None),
        P("ep", None, "et"),
        P("ep", "et", None),
    )
    out_specs = P("ep", "et")
    return jax.shard_map(
        per_device, mesh=mesh, in_specs=in_specs, out_specs=out_specs, check_vma=False
    )
```

```python
import functools

import jax
import jax.numpy as jnp
from jax import lax
from jax.experimental import pallas as pl
from jax.experimental.pallas import tpu as pltpu
from jax.sharding import PartitionSpec as P

MESH = pl.DeviceIdType.MESH
PAIR = 2
LANES = 128


def routed_layer(tokens, expert_ids, combine_numerators, expert_input, expert_output):
    ep_count = lax.axis_size("ep")
    group_rows = lax.all_gather(tokens, "et", axis=0, tiled=True)
    group_size = group_rows.shape[0]
    row_width = group_rows.shape[1]
    top_count = expert_ids.shape[1]
    capacity = 2 * max(1, group_size * top_count // ep_count)
    slot_total = ep_count * capacity
    numerators = combine_numerators.astype(jnp.float32)
    weights = 2.5 * numerators / jnp.sum(numerators, axis=1, keepdims=True)
    slot_expert = jnp.arange(ep_count, dtype=jnp.int32)
    matches = expert_ids[:, :, None] == slot_expert[None, None, :]
    picked = jnp.any(matches, axis=1).astype(jnp.int32)
    expert_weight = jnp.sum(jnp.where(matches, weights[:, :, None], jnp.float32(0.0)), axis=1)
    row = jnp.arange(group_size, dtype=jnp.int32)
    earlier = row[None, :] < row[:, None]
    slot_rank = jnp.sum(jnp.where(earlier[:, :, None], picked[None, :, :], 0), axis=1)
    placing = (slot_rank[:, :, None] == jnp.arange(capacity, dtype=jnp.int32)[None, None, :]) & (
        picked[:, :, None] > 0
    )
    placing = placing.reshape(group_size, slot_total)
    combiner = jnp.where(placing, jnp.repeat(expert_weight, capacity, axis=1), jnp.float32(0.0))
    outgoing = jnp.dot(
        placing.astype(jnp.bfloat16).T, group_rows, preferred_element_type=jnp.float32
    )
    outgoing = outgoing.astype(jnp.bfloat16).reshape(ep_count, capacity, row_width)
    incoming = lax.all_to_all(outgoing, "ep", split_axis=0, concat_axis=0, tiled=True)
    expert_rows = incoming.reshape(slot_total, row_width)
    input_proj = expert_input[0]
    output_proj = expert_output[0]
    projected = jnp.dot(expert_rows, input_proj, preferred_element_type=jnp.float32)
    hidden = jax.nn.silu(projected).astype(jnp.bfloat16)
    partial_out = jnp.dot(hidden, output_proj, preferred_element_type=jnp.float32)
    partial_out = partial_out.reshape(ep_count, capacity, output_proj.shape[1])
    expert_out = lax.psum_scatter(
        partial_out.astype(jnp.bfloat16), "et", scatter_dimension=2, tiled=True
    )
    share_width = expert_out.shape[2]
    returned = lax.all_to_all(expert_out, "ep", split_axis=0, concat_axis=0, tiled=True)
    returned = returned.reshape(slot_total, share_width).astype(jnp.float32)
    combined = jnp.dot(
        combiner, returned, precision=lax.Precision.HIGHEST, preferred_element_type=jnp.float32
    )
    return combined.astype(jnp.bfloat16)


def fused_kernel(
    line,
    size,
    ids_hbm,
    numerators_hbm,
    tokens_hbm,
    input_hbm,
    output_hbm,
    out_ref,
    ids_ref,
    numerators_ref,
    rows,
    input_proj,
    output_proj,
    part,
    core_in,
    core_sum,
    plane_in,
    line_out,
    line_in,
    weight_sem,
    own_sem,
    gather_send,
    gather_recv,
    core_send,
    core_recv,
    plane_send,
    plane_recv,
    line_send,
    line_recv,
):
    ep, x = lax.axis_index("ep"), lax.axis_index("et")
    c, y, z = ep % PAIR, (ep // PAIR) % PAIR, ep // (PAIR * PAIR)
    group, top = ids_ref.shape
    share, width = tokens_hbm.shape
    quarter = width // 4
    depth = input_hbm.shape[2]
    f32, bf16 = jnp.float32, jnp.bfloat16

    def at(c=c, y=y, z=z, x=x):
        return {"ep": (z * PAIR + y) * PAIR + c, "et": x}

    def across(step):
        place, bit = z, 1
        while bit <= step:
            if step & bit:
                place = place + bit - 2 * bit * ((z // bit) % 2)
            bit *= 2
        return place

    to_core, to_y, to_x, to_diagonal = at(c=1 - c), at(y=1 - y), at(x=1 - x), at(y=1 - y, x=1 - x)
    steps = range(1, line)
    z_of = {step: across(step) for step in steps}
    to_line = {step: at(z=z_of[step]) for step in steps}

    barrier = pltpu.get_barrier_semaphore()
    partners = [to_core, to_y, to_x, to_diagonal] + list(to_line.values())
    for partner in partners:
        pl.semaphore_signal(barrier, inc=1, device_id=partner, device_id_type=MESH)

    def slot(plane, c=c, y=y, x=x):
        return rows.at[plane // size, c, y, plane % size, x]

    own = slot(z)
    small = [
        pltpu.make_async_copy(ids_hbm, ids_ref, own_sem.at[0]),
        pltpu.make_async_copy(numerators_hbm, numerators_ref, own_sem.at[1]),
    ]
    load_own = pltpu.make_async_copy(tokens_hbm, own.at[:, pl.ds(LANES, width)], own_sem.at[2])
    for load in small + [load_own]:
        load.start()
    input_load = pltpu.make_async_copy(input_hbm.at[0], input_proj, weight_sem.at[0])
    input_load.start(priority=1)
    chunk_loads = []
    for hx in range(2):
        for p in range(2):
            load = pltpu.make_async_copy(
                output_hbm.at[0, :, pl.ds((2 * hx + p) * quarter, quarter)],
                output_proj.at[hx, p],
                weight_sem.at[1 + 2 * hx + p],
            )
            load.start(priority=1)
            chunk_loads.append(load)

    for load in small:
        load.wait()
    ids = ids_ref[...]
    numerators = numerators_ref[...]
    lane = lax.broadcasted_iota(jnp.int32, (group, LANES), 1)
    table = jnp.zeros((group, LANES), jnp.int32)
    for k in range(top):
        table = table + jnp.where(ids[:, k : k + 1] == lane, numerators[:, k : k + 1], 0)
    table = table.astype(f32)
    mine = table[:share]
    for step in range(1, group // share):
        mine = jnp.where(x == step, table[step * share : (step + 1) * share], mine)
    rows[z // size, c, y, z % size, x, :, :LANES] = mine.astype(bf16)

    load_own.wait()
    pl.semaphore_wait(barrier, len(partners))

    pending = []

    def send(src, dst, send_sem, recv_sem, partner):
        copy = pltpu.make_async_remote_copy(
            src_ref=src,
            dst_ref=dst,
            send_sem=send_sem,
            recv_sem=recv_sem,
            device_id=partner,
            device_id_type=MESH,
        )
        copy.start()
        return copy

    def sent(*copy):
        pending.append(send(*copy))

    def landed(block, send_sem, recv_sem):
        pltpu.make_async_remote_copy(
            src_ref=block,
            dst_ref=block,
            send_sem=send_sem,
            recv_sem=recv_sem,
            device_id=to_core,
            device_id_type=MESH,
        ).wait_recv()

    def gather_pair(kind, step):
        return gather_send.at[kind, step], gather_recv.at[kind, step]

    def spread(step):
        block = slot(step)
        for kind, partner in ((3, to_diagonal), (1, to_x), (2, to_y), (4, to_core)):
            sent(block, block, *gather_pair(kind, step), partner)

    def from_line(step):
        landed(slot(z_of[step]), *gather_pair(0, z_of[step]))
        spread(z_of[step])

    def to_other_core(step):
        for kind, block in (
            (1, slot(step, x=1 - x)),
            (2, slot(step, y=1 - y)),
            (3, slot(step, y=1 - y, x=1 - x)),
        ):
            landed(block, *gather_pair(kind, step))
            sent(block, block, *gather_pair(kind + 4, step), to_core)

    def gathered(step):
        for kind, block in (
            (4, slot(step, c=1 - c)),
            (5, slot(step, c=1 - c, x=1 - x)),
            (6, slot(step, c=1 - c, y=1 - y)),
            (7, slot(step, c=1 - c, y=1 - y, x=1 - x)),
        ):
            landed(block, *gather_pair(kind, step))

    count = line // size
    block_rows = size * group
    token_count = count * PAIR * PAIR * block_rows
    chunks = [(1 - x, 0), (x, 0), (1 - x, 1), (x, 1)]

    def compute():
        table = rows[..., :LANES].reshape(token_count, LANES).astype(f32)
        lane = lax.broadcasted_iota(jnp.int32, (token_count, LANES), 1)
        picked = jnp.sum(jnp.where(lane == ep, table, 0.0), axis=1, keepdims=True)
        weight = 2.5 * picked / jnp.sum(table, axis=1, keepdims=True)
        input_load.wait()
        taken = rows[..., LANES:].reshape(token_count, width)
        projected = jnp.dot(taken, input_proj[...], preferred_element_type=f32)
        hidden = jax.nn.silu(projected).astype(bf16)
        for load in chunk_loads:
            load.wait()
        for index, (hx, p) in enumerate(chunks):
            value = jnp.dot(hidden, output_proj[hx, p], preferred_element_type=f32)
            value = (value * weight).astype(bf16)
            for b in range(count):
                for cc in range(PAIR):
                    for yy in range(PAIR):
                        start = ((b * PAIR + cc) * PAIR + yy) * block_rows
                        part[b, cc, hx, p, yy] = value[start : start + block_rows]
            sent(
                part.at[:, 1 - c, hx, p],
                core_in.at[:, hx, p],
                core_send.at[0, hx, p],
                core_recv.at[0, hx, p],
                to_core,
            )

    def add_cores(b):
        for index, (hx, p) in enumerate(chunks):
            if b == 0:
                landed(core_in.at[:, hx, p], core_send.at[0, hx, p], core_recv.at[0, hx, p])
            core_sum[b, hx, p] = (
                part[b, c, hx, p].astype(f32) + core_in[b, hx, p].astype(f32)
            ).astype(bf16)
            wants = ((1, 1 - y, to_diagonal), (0, y, to_x)) if index % 2 == 0 else ((2, 1 - y, to_y),)
            for kind, yy, partner in wants:
                sent(
                    core_sum.at[b, hx, p, yy],
                    plane_in.at[b, kind, p],
                    plane_send.at[b, kind, p],
                    plane_recv.at[b, kind, p],
                    partner,
                )

    def add_plane(b, p):
        total = core_sum[b, x, p, y].astype(f32)
        for kind in range(3):
            landed(plane_in.at[b, kind, p], plane_send.at[b, kind, p], plane_recv.at[b, kind, p])
            total = total + plane_in[b, kind, p].astype(f32)
        for i in range(size):
            plane = b * size + i
            line_out[plane, p] = total[i * group : (i + 1) * group].astype(bf16)

            @pl.when(plane != z)
            def _():
                home(plane, p).start()

    def home(plane, p):
        return pltpu.make_async_remote_copy(
            src_ref=line_out.at[plane, p],
            dst_ref=line_in.at[z, p],
            send_sem=line_send.at[plane, p],
            recv_sem=line_recv.at[z, p],
            device_id=at(z=plane),
            device_id_type=MESH,
        )

    low = (2 * z < line).astype(jnp.int32)
    for k in range(line - 1):
        value = line - 1 - k
        down, up = value - (value <= z).astype(jnp.int32), k + (k >= z).astype(jnp.int32)
        far = low * down + (1 - low) * up
        sent(own, own, gather_send.at[0, k], gather_recv.at[0, z], at(z=far))
    spread(z)
    near = [z] + [z_of[step] for step in steps]
    for step in steps:
        from_line(step)
    for plane in near:
        to_other_core(plane)
    for plane in near:
        gathered(plane)
    compute()
    def first_plane():
        for p in range(2):
            add_plane(0, p)

    for b in range(count):
        add_cores(b)
        if b == 0:
            pl.when(c == 1)(first_plane)
    pl.when(c == 0)(first_plane)
    for b in range(1, count):
        for p in range(2):
            add_plane(b, p)
    for p in range(2):
        total = line_out[z, p].astype(f32)
        for step in steps:
            other = z_of[step]
            landed(line_in.at[other, p], line_send.at[other, p], line_recv.at[other, p])
            total = total + line_in[other, p].astype(f32)
        out_ref[:, p * quarter : (p + 1) * quarter] = total.astype(bf16)
    for copy in pending:
        copy.wait_send()
    for step in steps:
        for p in range(2):
            home(z_of[step], p).wait_send()


def fused_layer(tokens, expert_ids, combine_numerators, expert_input, expert_output):
    line = lax.axis_size("ep") // (PAIR * PAIR)
    share, width = tokens.shape
    group = expert_ids.shape[0]
    half, quarter = width // 2, width // 4
    depth = expert_input.shape[2]
    count, size = line, 1
    block_rows = size * group
    bf16 = jnp.bfloat16
    dma = pltpu.SemaphoreType.DMA
    stay = pl.BlockSpec(memory_space=pl.ANY)
    return pl.pallas_call(
        functools.partial(fused_kernel, line, size),
        out_shape=pltpu.VMEM((group, half), bf16),
        in_specs=[stay] * 5,
        out_specs=pl.BlockSpec(memory_space=pltpu.VMEM),
        scratch_shapes=[
            pltpu.VMEM(expert_ids.shape, expert_ids.dtype),
            pltpu.VMEM(combine_numerators.shape, combine_numerators.dtype),
            pltpu.VMEM((count, PAIR, PAIR, size, 2, share, LANES + width), bf16),
            pltpu.VMEM((width, depth), bf16),
            pltpu.VMEM((2, 2, depth, quarter), bf16),
            pltpu.VMEM((count, PAIR, 2, 2, PAIR, block_rows, quarter), bf16),
            pltpu.VMEM((count, 2, 2, PAIR, block_rows, quarter), bf16),
            pltpu.VMEM((count, 2, 2, PAIR, block_rows, quarter), bf16),
            pltpu.VMEM((count, 3, 2, block_rows, quarter), bf16),
            pltpu.VMEM((line, 2, group, quarter), bf16),
            pltpu.VMEM((line, 2, group, quarter), bf16),
            dma((5,)),
            dma((3,)),
            dma((8, line)),
            dma((8, line)),
            dma((count, 2, 2)),
            dma((count, 2, 2)),
            dma((count, 3, 2)),
            dma((count, 3, 2)),
            dma((line, 2)),
            dma((line, 2)),
        ],
        compiler_params=pltpu.CompilerParams(
            collective_id=0, has_side_effects=True, vmem_limit_bytes=60 * 1024 * 1024
        ),
    )(expert_ids, combine_numerators, tokens, expert_input, expert_output)


def per_device(tokens, expert_ids, combine_numerators, expert_input, expert_output):
    ep_count, et_count = lax.axis_size("ep"), lax.axis_size("et")
    group, top = expert_ids.shape
    capacity = 2 * max(1, group * top // ep_count)
    line = ep_count // (PAIR * PAIR)
    dense = group <= capacity and et_count == 2 and ep_count == PAIR * PAIR * line
    dense = dense and line > 1 and line & (line - 1) == 0
    run = fused_layer if dense and ep_count <= LANES else routed_layer
    return run(tokens, expert_ids, combine_numerators, expert_input, expert_output)


def solution(mesh):
    in_specs = (
        P(("ep", "et"), None),
        P("ep", None),
        P("ep", None),
        P("ep", None, "et"),
        P("ep", "et", None),
    )
    out_specs = P("ep", "et")
    return jax.shard_map(
        per_device, mesh=mesh, in_specs=in_specs, out_specs=out_specs, check_vma=False
    )
```

```python
import functools

import jax
import jax.numpy as jnp
from jax import lax
from jax.experimental import pallas as pl
from jax.experimental.pallas import tpu as pltpu
from jax.sharding import PartitionSpec as P

MESH = pl.DeviceIdType.MESH
PAIR = 2
LANES = 128


def routed_layer(tokens, expert_ids, combine_numerators, expert_input, expert_output):
    ep_count = lax.axis_size("ep")
    group_rows = lax.all_gather(tokens, "et", axis=0, tiled=True)
    group_size = group_rows.shape[0]
    row_width = group_rows.shape[1]
    top_count = expert_ids.shape[1]
    capacity = 2 * max(1, group_size * top_count // ep_count)
    slot_total = ep_count * capacity
    numerators = combine_numerators.astype(jnp.float32)
    weights = 2.5 * numerators / jnp.sum(numerators, axis=1, keepdims=True)
    slot_expert = jnp.arange(ep_count, dtype=jnp.int32)
    matches = expert_ids[:, :, None] == slot_expert[None, None, :]
    picked = jnp.any(matches, axis=1).astype(jnp.int32)
    expert_weight = jnp.sum(jnp.where(matches, weights[:, :, None], jnp.float32(0.0)), axis=1)
    row = jnp.arange(group_size, dtype=jnp.int32)
    earlier = row[None, :] < row[:, None]
    slot_rank = jnp.sum(jnp.where(earlier[:, :, None], picked[None, :, :], 0), axis=1)
    placing = (slot_rank[:, :, None] == jnp.arange(capacity, dtype=jnp.int32)[None, None, :]) & (
        picked[:, :, None] > 0
    )
    placing = placing.reshape(group_size, slot_total)
    combiner = jnp.where(placing, jnp.repeat(expert_weight, capacity, axis=1), jnp.float32(0.0))
    outgoing = jnp.dot(
        placing.astype(jnp.bfloat16).T, group_rows, preferred_element_type=jnp.float32
    )
    outgoing = outgoing.astype(jnp.bfloat16).reshape(ep_count, capacity, row_width)
    incoming = lax.all_to_all(outgoing, "ep", split_axis=0, concat_axis=0, tiled=True)
    expert_rows = incoming.reshape(slot_total, row_width)
    input_proj = expert_input[0]
    output_proj = expert_output[0]
    projected = jnp.dot(expert_rows, input_proj, preferred_element_type=jnp.float32)
    hidden = jax.nn.silu(projected).astype(jnp.bfloat16)
    partial_out = jnp.dot(hidden, output_proj, preferred_element_type=jnp.float32)
    partial_out = partial_out.reshape(ep_count, capacity, output_proj.shape[1])
    expert_out = lax.psum_scatter(
        partial_out.astype(jnp.bfloat16), "et", scatter_dimension=2, tiled=True
    )
    share_width = expert_out.shape[2]
    returned = lax.all_to_all(expert_out, "ep", split_axis=0, concat_axis=0, tiled=True)
    returned = returned.reshape(slot_total, share_width).astype(jnp.float32)
    combined = jnp.dot(
        combiner, returned, precision=lax.Precision.HIGHEST, preferred_element_type=jnp.float32
    )
    return combined.astype(jnp.bfloat16)


def fused_kernel(
    line,
    size,
    ids_hbm,
    numerators_hbm,
    tokens_hbm,
    input_hbm,
    output_hbm,
    out_ref,
    ids_ref,
    numerators_ref,
    rows,
    input_proj,
    output_proj,
    part,
    core_in,
    core_sum,
    plane_in,
    line_out,
    line_in,
    weight_sem,
    own_sem,
    gather_send,
    gather_recv,
    core_send,
    core_recv,
    plane_send,
    plane_recv,
    line_send,
    line_recv,
):
    ep, x = lax.axis_index("ep"), lax.axis_index("et")
    c, y, z = ep % PAIR, (ep // PAIR) % PAIR, ep // (PAIR * PAIR)
    group, top = ids_ref.shape
    share, width = tokens_hbm.shape
    quarter = width // 4
    depth = input_hbm.shape[2]
    f32, bf16 = jnp.float32, jnp.bfloat16

    def at(c=c, y=y, z=z, x=x):
        return {"ep": (z * PAIR + y) * PAIR + c, "et": x}

    def across(step):
        place, bit = z, 1
        while bit <= step:
            if step & bit:
                place = place + bit - 2 * bit * ((z // bit) % 2)
            bit *= 2
        return place

    to_core, to_y, to_x, to_diagonal = at(c=1 - c), at(y=1 - y), at(x=1 - x), at(y=1 - y, x=1 - x)
    steps = range(1, line)
    z_of = {step: across(step) for step in steps}
    to_line = {step: at(z=z_of[step]) for step in steps}

    barrier = pltpu.get_barrier_semaphore()
    partners = [to_core, to_y, to_x, to_diagonal] + list(to_line.values())
    for partner in partners:
        pl.semaphore_signal(barrier, inc=1, device_id=partner, device_id_type=MESH)

    def slot(plane, c=c, y=y, x=x):
        return rows.at[plane // size, c, y, plane % size, x]

    own = slot(z)
    small = [
        pltpu.make_async_copy(ids_hbm, ids_ref, own_sem.at[0]),
        pltpu.make_async_copy(numerators_hbm, numerators_ref, own_sem.at[1]),
    ]
    load_own = pltpu.make_async_copy(tokens_hbm, own.at[:, pl.ds(LANES, width)], own_sem.at[2])
    for load in small + [load_own]:
        load.start()
    input_load = pltpu.make_async_copy(input_hbm.at[0], input_proj, weight_sem.at[0])
    input_load.start(priority=1)
    chunk_loads = []
    for hx in range(2):
        for p in range(2):
            load = pltpu.make_async_copy(
                output_hbm.at[0, :, pl.ds((2 * hx + p) * quarter, quarter)],
                output_proj.at[hx, p],
                weight_sem.at[1 + 2 * hx + p],
            )
            load.start(priority=1)
            chunk_loads.append(load)

    for load in small:
        load.wait()
    ids = ids_ref[...]
    numerators = numerators_ref[...]
    lane = lax.broadcasted_iota(jnp.int32, (group, LANES), 1)
    table = jnp.zeros((group, LANES), jnp.int32)
    for k in range(top):
        table = table + jnp.where(ids[:, k : k + 1] == lane, numerators[:, k : k + 1], 0)
    table = table.astype(f32)
    mine = table[:share]
    for step in range(1, group // share):
        mine = jnp.where(x == step, table[step * share : (step + 1) * share], mine)
    rows[z // size, c, y, z % size, x, :, :LANES] = mine.astype(bf16)

    load_own.wait()
    pl.semaphore_wait(barrier, len(partners))

    pending = []

    def send(src, dst, send_sem, recv_sem, partner):
        copy = pltpu.make_async_remote_copy(
            src_ref=src,
            dst_ref=dst,
            send_sem=send_sem,
            recv_sem=recv_sem,
            device_id=partner,
            device_id_type=MESH,
        )
        copy.start()
        return copy

    def sent(*copy):
        pending.append(send(*copy))

    def landed(block, send_sem, recv_sem):
        pltpu.make_async_remote_copy(
            src_ref=block,
            dst_ref=block,
            send_sem=send_sem,
            recv_sem=recv_sem,
            device_id=to_core,
            device_id_type=MESH,
        ).wait_recv()

    def gather_pair(kind, step):
        return gather_send.at[kind, step], gather_recv.at[kind, step]

    def spread(step):
        block = slot(step)
        for kind, partner in ((3, to_diagonal), (1, to_x), (2, to_y), (4, to_core)):
            sent(block, block, *gather_pair(kind, step), partner)

    def from_line(step):
        landed(slot(z_of[step]), *gather_pair(0, z_of[step]))
        spread(z_of[step])

    def to_other_core(step):
        for kind, block in (
            (1, slot(step, x=1 - x)),
            (2, slot(step, y=1 - y)),
            (3, slot(step, y=1 - y, x=1 - x)),
        ):
            landed(block, *gather_pair(kind, step))
            sent(block, block, *gather_pair(kind + 4, step), to_core)

    def gathered(step):
        for kind, block in (
            (4, slot(step, c=1 - c)),
            (5, slot(step, c=1 - c, x=1 - x)),
            (6, slot(step, c=1 - c, y=1 - y)),
            (7, slot(step, c=1 - c, y=1 - y, x=1 - x)),
        ):
            landed(block, *gather_pair(kind, step))

    count = line // size
    block_rows = size * group
    token_count = count * PAIR * PAIR * block_rows
    chunks = [(1 - x, 0), (x, 0), (1 - x, 1), (x, 1)]

    def compute():
        table = rows[..., :LANES].reshape(token_count, LANES).astype(f32)
        lane = lax.broadcasted_iota(jnp.int32, (token_count, LANES), 1)
        picked = jnp.sum(jnp.where(lane == ep, table, 0.0), axis=1, keepdims=True)
        weight = 2.5 * picked / jnp.sum(table, axis=1, keepdims=True)
        input_load.wait()
        taken = rows[..., LANES:].reshape(token_count, width)
        projected = jnp.dot(taken, input_proj[...], preferred_element_type=f32)
        hidden = (jax.nn.silu(projected) * weight).astype(bf16)
        for load in chunk_loads:
            load.wait()
        for index, (hx, p) in enumerate(chunks):
            value = jnp.dot(hidden, output_proj[hx, p], preferred_element_type=f32)
            value = value.astype(bf16)
            for b in range(count):
                for cc in range(PAIR):
                    for yy in range(PAIR):
                        start = ((b * PAIR + cc) * PAIR + yy) * block_rows
                        part[b, cc, hx, p, yy] = value[start : start + block_rows]
            sent(
                part.at[:, 1 - c, hx, p],
                core_in.at[:, hx, p],
                core_send.at[0, hx, p],
                core_recv.at[0, hx, p],
                to_core,
            )

    def add_cores(b):
        for index, (hx, p) in enumerate(chunks):
            if b == 0:
                landed(core_in.at[:, hx, p], core_send.at[0, hx, p], core_recv.at[0, hx, p])
            core_sum[b, hx, p] = (
                part[b, c, hx, p].astype(f32) + core_in[b, hx, p].astype(f32)
            ).astype(bf16)
            wants = ((1, 1 - y, to_diagonal), (0, y, to_x)) if index % 2 == 0 else ((2, 1 - y, to_y),)
            for kind, yy, partner in wants:
                sent(
                    core_sum.at[b, hx, p, yy],
                    plane_in.at[b, kind, p],
                    plane_send.at[b, kind, p],
                    plane_recv.at[b, kind, p],
                    partner,
                )

    def add_plane(b, p):
        total = core_sum[b, x, p, y].astype(f32)
        for kind in range(3):
            landed(plane_in.at[b, kind, p], plane_send.at[b, kind, p], plane_recv.at[b, kind, p])
            total = total + plane_in[b, kind, p].astype(f32)
        for i in range(size):
            plane = b * size + i
            line_out[plane, p] = total[i * group : (i + 1) * group].astype(bf16)

            @pl.when(plane != z)
            def _():
                home(plane, p).start()

    def home(plane, p):
        return pltpu.make_async_remote_copy(
            src_ref=line_out.at[plane, p],
            dst_ref=line_in.at[z, p],
            send_sem=line_send.at[plane, p],
            recv_sem=line_recv.at[z, p],
            device_id=at(z=plane),
            device_id_type=MESH,
        )

    low = (2 * z < line).astype(jnp.int32)
    for k in range(line - 1):
        value = line - 1 - k
        down, up = value - (value <= z).astype(jnp.int32), k + (k >= z).astype(jnp.int32)
        far = low * down + (1 - low) * up
        sent(own, own, gather_send.at[0, k], gather_recv.at[0, z], at(z=far))
    spread(z)
    near = [z] + [z_of[step] for step in steps]
    for step in steps:
        from_line(step)
    for plane in near:
        to_other_core(plane)
    for plane in near:
        gathered(plane)
    compute()
    def first_plane():
        for p in range(2):
            add_plane(0, p)

    for b in range(count):
        add_cores(b)
        if b == 0:
            pl.when(c == 1)(first_plane)
    pl.when(c == 0)(first_plane)
    for b in range(1, count):
        for p in range(2):
            add_plane(b, p)
    for copy in pending:
        copy.wait_send()
    for p in range(2):
        total = line_out[z, p].astype(f32)
        for step in steps:
            other = z_of[step]
            landed(line_in.at[other, p], line_send.at[other, p], line_recv.at[other, p])
            total = total + line_in[other, p].astype(f32)
        out_ref[:, p * quarter : (p + 1) * quarter] = total.astype(bf16)
    for step in steps:
        for p in range(2):
            home(z_of[step], p).wait_send()


def fused_layer(tokens, expert_ids, combine_numerators, expert_input, expert_output):
    line = lax.axis_size("ep") // (PAIR * PAIR)
    share, width = tokens.shape
    group = expert_ids.shape[0]
    half, quarter = width // 2, width // 4
    depth = expert_input.shape[2]
    count, size = line, 1
    block_rows = size * group
    bf16 = jnp.bfloat16
    dma = pltpu.SemaphoreType.DMA
    stay = pl.BlockSpec(memory_space=pl.ANY)
    return pl.pallas_call(
        functools.partial(fused_kernel, line, size),
        out_shape=pltpu.VMEM((group, half), bf16),
        in_specs=[stay] * 5,
        out_specs=pl.BlockSpec(memory_space=pltpu.VMEM),
        scratch_shapes=[
            pltpu.VMEM(expert_ids.shape, expert_ids.dtype),
            pltpu.VMEM(combine_numerators.shape, combine_numerators.dtype),
            pltpu.VMEM((count, PAIR, PAIR, size, 2, share, LANES + width), bf16),
            pltpu.VMEM((width, depth), bf16),
            pltpu.VMEM((2, 2, depth, quarter), bf16),
            pltpu.VMEM((count, PAIR, 2, 2, PAIR, block_rows, quarter), bf16),
            pltpu.VMEM((count, 2, 2, PAIR, block_rows, quarter), bf16),
            pltpu.VMEM((count, 2, 2, PAIR, block_rows, quarter), bf16),
            pltpu.VMEM((count, 3, 2, block_rows, quarter), bf16),
            pltpu.VMEM((line, 2, group, quarter), bf16),
            pltpu.VMEM((line, 2, group, quarter), bf16),
            dma((5,)),
            dma((3,)),
            dma((8, line)),
            dma((8, line)),
            dma((count, 2, 2)),
            dma((count, 2, 2)),
            dma((count, 3, 2)),
            dma((count, 3, 2)),
            dma((line, 2)),
            dma((line, 2)),
        ],
        compiler_params=pltpu.CompilerParams(
            collective_id=0, has_side_effects=True, vmem_limit_bytes=60 * 1024 * 1024
        ),
    )(expert_ids, combine_numerators, tokens, expert_input, expert_output)


def per_device(tokens, expert_ids, combine_numerators, expert_input, expert_output):
    ep_count, et_count = lax.axis_size("ep"), lax.axis_size("et")
    group, top = expert_ids.shape
    capacity = 2 * max(1, group * top // ep_count)
    line = ep_count // (PAIR * PAIR)
    dense = group <= capacity and et_count == 2 and ep_count == PAIR * PAIR * line
    dense = dense and line > 1 and line & (line - 1) == 0
    run = fused_layer if dense and ep_count <= LANES else routed_layer
    return run(tokens, expert_ids, combine_numerators, expert_input, expert_output)


def solution(mesh):
    in_specs = (
        P(("ep", "et"), None),
        P("ep", None),
        P("ep", None),
        P("ep", None, "et"),
        P("ep", "et", None),
    )
    out_specs = P("ep", "et")
    return jax.shard_map(
        per_device, mesh=mesh, in_specs=in_specs, out_specs=out_specs, check_vma=False
    )
```
